32 devices in a mesh: shot: 4 (over y, core), depth: 8 (over z, x).
Axes of the slice: x: 2, y: 2, z: 4, core: 2. Of those that a mesh axis runs over, the one named last changes fastest.
Arguments:
- grad_part: float32 [4, 256, 8192], P('shot', 'depth'), may hold values from -6 to 6
- illum_part: float32 [4, 256, 8192], P('shot', 'depth'), may hold values from 0.1 to 1
- source_count: int32 [4], P('shot'), may hold values from 1 to 8
- rate: float32 [8192], P('shot'), may hold values from 0.00078125 to 0.03
- coef_table: float32 [64], replicated, may hold values from 0.2 to 1
- coef_index: int32 [256], P('depth'), may hold values from 0 to 63
Outputs:
- image: float32 [256, 8192], P('depth', 'shot')
The draws below stay inside these ranges and needn't reach their ends.
All inputs are finite; a program needn't handle non-finite values.
Results may differ from the reference program's by a relative error of at most 0.0003.
Values sent between devices are 32-bit elements; how exact they have to be, the bound alone decides.
A program may use at most 64 MiB of HBM per device.

```python
import math
import jax
import jax.numpy as jnp
from jax import lax

LAT = 8192
SRC = 8
NTAB = 64
NZ = 256
GROUPS = 4


def with_ends(array, own_key, low, top_value):
    index_at = [jax.random.randint(jax.random.fold_in(own_key, axis), (), 0, length) for axis, length in enumerate(array.shape)]
    main_axis = array.shape.index(max(array.shape))
    neighbour = index_at[:main_axis] + [(index_at[main_axis] + 1) % array.shape[main_axis]] + index_at[main_axis + 1:]
    return array.at[tuple(index_at)].set(low).at[tuple(neighbour)].set(top_value)


def spiked(result, key, source, target, shards_of, factor):
    owner, partner = [(jnp.arange(result.shape[axis_at]) // (result.shape[axis_at] // shards_of)).reshape([-1 if axis == axis_at else 1 for axis in range(result.ndim)]) for axis_at in (source, target)]
    chosen = jax.random.permutation(key, shards_of)[partner]
    strong = (owner == chosen) | (owner == (partner + shards_of // 2) % shards_of)
    return jnp.where(strong, factor * result, result)


def level_of(rng, shape, shards, low, largest):
    level, own = 1.0, jax.random.fold_in(rng, 6)
    for position, shards_of in shards:
        draws = jnp.exp(jax.random.uniform(jax.random.fold_in(own, position), (shards_of,), jnp.float32, low / len(shards), largest / len(shards)))
        level = level * jnp.repeat(draws, shape[position] // shards_of).reshape([-1 if axis == position else 1 for axis in range(len(shape))])
    return level


def noise_with(stream_key, shape, scale, limit, pieces, heavy, held_as=jnp.bfloat16):
    drawn = scale * jax.random.normal(stream_key, shape, jnp.float32)
    if pieces:
        drawn = drawn * level_of(stream_key, shape, pieces, -0.22, 0.18)
    return jnp.clip(spiked(drawn, jax.random.fold_in(stream_key, 3), *heavy), -limit, limit).astype(held_as)


def setup_inputs(seed: int = 0) -> dict:
    arg_keys = jax.random.split(jax.random.key(seed), 7)
    grad_part = noise_with(arg_keys[0], (GROUPS, NZ, LAT), 1.0, 6.0, ((0, 4), (1, 8)), (0, 2, 4, 2.0), jnp.float32)
    illum_part = jnp.clip(jnp.exp(math.log(1.0) - 2.3025851 * jax.random.uniform(arg_keys[1], (GROUPS, NZ, LAT), jnp.float32) ** level_of(arg_keys[1], (GROUPS, NZ, LAT), ((0, 4), (1, 8)), -0.2, 0.2)), 0.1, 1.0)
    source_count = with_ends(jax.random.randint(arg_keys[2], (GROUPS,), 1, SRC + 1), jax.random.fold_in(arg_keys[2], 1), 1, SRC).astype(jnp.int32)
    rate = jnp.clip(jnp.exp(math.log(0.03) - 3.6480574 * jax.random.uniform(arg_keys[3], (LAT,), jnp.float32) ** level_of(arg_keys[3], (LAT,), ((0, 4),), -0.2, 0.2)), 0.00078125, 0.03)
    coef_table = jnp.clip(jnp.exp(jax.random.uniform(arg_keys[4], (NTAB,), jnp.float32, math.log(0.2), math.log(1.0))), 0.2, 1.0)
    coef_index = with_ends(jax.random.randint(arg_keys[5], (NZ,), 0, NTAB), jax.random.fold_in(arg_keys[5], 1), 0, NTAB - 1).astype(jnp.int32)
    return {"grad_part": grad_part, "illum_part": illum_part, "source_count": source_count, "rate": rate, "coef_table": coef_table, "coef_index": coef_index}


def combine(earlier, later):
    return (earlier[0] * later[0], later[0] * earlier[1] + later[1])


def reference(grad_part, illum_part, source_count, rate, coef_table, coef_index):
    weight = 1.0 / source_count.astype(jnp.float32)
    scaled = grad_part * weight[:, None, None]
    summed = jnp.sum(scaled, axis=0)
    lights = jnp.sum(illum_part, axis=0)
    quotient = summed / lights
    picked = coef_table[coef_index]
    factor = jnp.exp(-(picked[:, None] * rate[None, :]))
    _, smooth = lax.associative_scan(combine, (factor, (1.0 - factor) * quotient), axis=0)
    _, image = lax.associative_scan(combine, (factor, (1.0 - factor) * smooth), reverse=True, axis=0)
    return image
```

```python
import functools

import jax
import jax.numpy as jnp
from jax import lax
from jax.experimental import pallas as pl
from jax.experimental.pallas import tpu as pltpu
from jax.sharding import PartitionSpec as P

MESH = pl.DeviceIdType.MESH
LANES = 128
SUB = 8


def body(
    dims,
    grad, illum, count, rate, table, index, out,
    own, part, sums, landed, early, late, inject, weigh, back, reach, held, states, weights,
    own_sem, part_send, part_recv, sums_send, sums_recv,
    early_send, early_recv, late_send, late_recv, w_send, w_recv,
):
    ys, ks, rows, width, chunks = dims
    cw = width // chunks
    cols = cw // LANES
    tiles = rows // SUB
    me = lax.axis_index("shot")
    d = lax.axis_index("depth")
    y, c = me // 2, me % 2
    mate = y * 2 + 1 - c

    def peer(i):
        return lax.rem(d + i, ks)

    def other(i):
        return lax.rem(y + i, ys)

    barrier = pltpu.get_barrier_semaphore()
    pl.semaphore_signal(barrier, inc=1, device_id=(mate, d), device_id_type=MESH)
    for i in range(1, ys):
        pl.semaphore_signal(barrier, inc=1, device_id=(other(i) * 2 + c, d), device_id_type=MESH)
    for i in range(1, ks):
        pl.semaphore_signal(barrier, inc=1, device_id=(me, peer(i)), device_id_type=MESH)

    def slab(src, target, core, ch):
        at = pl.multiple_of((target * 2 + core) * width + ch * cw, LANES)
        return src.at[0, :, pl.ds(at, cw)]

    order = [(i, ch) for i in [*range(1, ys), 0] for ch in range(chunks)]

    def own_copy(i, ch, a):
        return pltpu.make_async_copy(
            slab((grad, illum)[a], other(i), c, ch), own.at[i, ch, a], own_sem.at[i, ch, a]
        )

    def part_copy(i, ch, a):
        return pltpu.make_async_remote_copy(
            src_ref=slab((grad, illum)[a], other(i), 1 - c, ch),
            dst_ref=part.at[i, ch, a],
            send_sem=part_send.at[i, ch, a],
            recv_sem=part_recv.at[i, ch, a],
            device_id=(mate, d),
            device_id_type=MESH,
        )

    def sums_copy(i, ch):
        return pltpu.make_async_remote_copy(
            src_ref=sums.at[i - 1, ch],
            dst_ref=landed.at[i - 1, ch],
            send_sem=sums_send.at[i - 1, ch],
            recv_sem=sums_recv.at[i - 1, ch],
            device_id=(other(i) * 2 + c, d),
            device_id_type=MESH,
        )

    def early_copy(i):
        return pltpu.make_async_remote_copy(
            src_ref=early.at[0],
            dst_ref=early.at[ks - i],
            send_sem=early_send.at[i - 1],
            recv_sem=early_recv.at[ks - i - 1],
            device_id=(me, peer(i)),
            device_id_type=MESH,
        )

    def late_copy(i, ch):
        return pltpu.make_async_remote_copy(
            src_ref=late.at[0, ch],
            dst_ref=late.at[ks - i, ch],
            send_sem=late_send.at[i - 1, ch],
            recv_sem=late_recv.at[ks - i - 1, ch],
            device_id=(me, peer(i)),
            device_id_type=MESH,
        )

    w_copy = pltpu.make_async_remote_copy(
        src_ref=weights.at[0],
        dst_ref=weights.at[1],
        send_sem=w_send,
        recv_sem=w_recv,
        device_id=(mate, d),
        device_id_type=MESH,
    )

    for i, ch in order:
        for a in range(2):
            own_copy(i, ch, a).start()
    weights[0] = 1.0 / jnp.full((SUB, LANES), count[0], jnp.int32).astype(jnp.float32)

    pl.semaphore_wait(barrier, ys + ks - 1)
    w_copy.start()
    for i, ch in order:
        for a in range(2):
            part_copy(i, ch, a).start()

    sub = lax.broadcasted_iota(jnp.int32, (SUB, LANES), 0)

    def prefix(v):
        for s in (1, 2, 4):
            v = v + jnp.where(sub >= s, pltpu.roll(v, s, 0), 0.0)
        return v

    def suffix(v):
        for s in (1, 2, 4):
            v = v + jnp.where(sub < SUB - s, pltpu.roll(v, SUB - s, 0), 0.0)
        return v

    def first(v):
        return jnp.broadcast_to(v[0:1], (SUB, LANES))

    def last(v):
        return jnp.broadcast_to(v[SUB - 1 : SUB], (SUB, LANES))

    coef, through, before = [], [], []
    total = jnp.zeros((SUB, LANES), jnp.float32)
    for t in range(tiles):
        v = jnp.zeros((SUB, LANES), jnp.float32)
        for r in range(SUB):
            v = jnp.where(sub == r, table[index[t * SUB + r]], v)
        run = prefix(v) + total
        coef.append(v)
        through.append(run)
        before.append(run - v)
        total = last(run)

    def terms():
        for j in range(width // LANES):
            at = pl.ds(j * LANES, LANES)
            ch, jj = j // cols, j % cols
            r = jnp.broadcast_to(rate[0:1, at], (SUB, LANES))
            tail = jnp.zeros((SUB, LANES), jnp.float32)
            for t in reversed(range(tiles)):
                zs = pl.ds(t * SUB, SUB)
                rest = 1.0 - jnp.exp(-(coef[t] * r))
                inject[zs, at] = rest * jnp.exp(through[t] * r)
                h = rest * jnp.exp(-((through[t] + before[t]) * r))
                weigh[zs, at] = h
                lift = jnp.exp(before[t] * r)
                back[zs, at] = lift
                run = suffix(h) + tail
                reach[zs, at] = lift * run
                tail = first(run)
            early[0, 0, pl.ds(j, 1), :] = jnp.exp(-(total * r))[0:1]
            early[0, 1, pl.ds(j, 1), :] = tail[0:1]

    def reduced(i, ch, a, zs, at):
        if a == 0:
            w, v = weights[0], weights[1]
            return own[i, ch, 0, zs, at] * w + part[i, ch, 0, zs, at] * v
        return own[i, ch, 1, zs, at] + part[i, ch, 1, zs, at]

    def arrived(i, ch):
        for a in range(2):
            own_copy(i, ch, a).wait()
            part_copy(i, ch, a).wait_recv()

    w_copy.wait_recv()
    for n, (i, ch) in enumerate(order[: (ys - 1) * chunks]):
        arrived(i, ch)
        for j in range(cols):
            at = pl.ds(j * LANES, LANES)
            for t in range(tiles):
                zs = pl.ds(t * SUB, SUB)
                for a in range(2):
                    sums[i - 1, ch, a, zs, at] = reduced(i, ch, a, zs, at)
        sums_copy(i, ch).start()

    terms()
    for i in range(1, ks):
        early_copy(i).start()

    for ch in range(chunks):
        arrived(0, ch)
        for i in range(1, ys):
            sums_copy(i, ch).wait_recv()
        for j in range(cols):
            at = pl.ds(j * LANES, LANES)
            full = pl.ds(ch * cw + j * LANES, LANES)
            carry = jnp.zeros((SUB, LANES), jnp.float32)
            parts = []
            for t in range(tiles):
                zs = pl.ds(t * SUB, SUB)
                num, den = reduced(0, ch, 0, zs, at), reduced(0, ch, 1, zs, at)
                for i in range(1, ys):
                    num = num + landed[i - 1, ch, 0, zs, at]
                    den = den + landed[i - 1, ch, 1, zs, at]
                run = prefix(inject[zs, full] * (num / den)) + carry
                parts.append(run)
                carry = last(run)
            row = pl.ds(ch * cols + j, 1)
            late[0, ch, 0, pl.ds(j, 1), :] = carry[0:1] * early[0, 0, row, :]
            tail = jnp.zeros((SUB, LANES), jnp.float32)
            for t in reversed(range(tiles)):
                zs = pl.ds(t * SUB, SUB)
                run = suffix(weigh[zs, full] * parts[t]) + tail
                held[zs, full] = run
                tail = first(run)
            late[0, ch, 1, pl.ds(j, 1), :] = tail[0:1]
        for i in range(1, ks):
            late_copy(i, ch).start()

    for i in range(1, ks):
        early_copy(i).wait_recv()

    for ch in range(chunks):
        for i in range(1, ks):
            late_copy(i, ch).wait_recv()
        rs = pl.ds(ch * cols, cols)
        state = jnp.zeros((cols, LANES), jnp.float32)
        mine = state
        ups = []
        for k in range(ks):
            slot = lax.rem(k - d + ks, ks)
            mine = jnp.where(k == d, state, mine)
            ups.append(late[slot, ch, 1] + early[slot, 1, rs] * state)
            if k < ks - 1:
                state = late[slot, ch, 0] + early[slot, 0, rs] * state
        up = jnp.zeros((cols, LANES), jnp.float32)
        for k in reversed(range(1, ks)):
            slot = lax.rem(k - d + ks, ks)
            up = jnp.where(k > d, ups[k] + early[slot, 0, rs] * up, up)
        states[0, rs] = mine
        states[1, rs] = up * early[0, 0, rs]
        for j in range(cols):
            row = pl.ds(ch * cols + j, 1)
            full = pl.ds(ch * cw + j * LANES, LANES)
            e = jnp.broadcast_to(states[0, row, :], (SUB, LANES))
            b = jnp.broadcast_to(states[1, row, :], (SUB, LANES))
            for t in range(tiles):
                zs = pl.ds(t * SUB, SUB)
                out[zs, full] = back[zs, full] * (held[zs, full] + b) + reach[zs, full] * e

    w_copy.wait_send()
    for i, ch in order:
        for a in range(2):
            part_copy(i, ch, a).wait_send()
        if i:
            sums_copy(i, ch).wait_send()
    for i in range(1, ks):
        early_copy(i).wait_send()
        for ch in range(chunks):
            late_copy(i, ch).wait_send()


def shards(ys, ks, grad_part, illum_part, source_count, rate, coef_table, coef_index):
    _, rows, lateral = grad_part.shape
    width = lateral // (2 * ys)
    chunks = min(4, width // LANES)
    cw = width // chunks
    cols = cw // LANES
    f32 = jnp.float32
    dma = pltpu.SemaphoreType.DMA
    blocks = (ys, chunks, 2, rows, cw)
    peers = (ys - 1, chunks, 2, rows, cw)
    field = pltpu.VMEM((rows, width), f32)
    anywhere = pl.BlockSpec(memory_space=pl.ANY)
    scalars = pl.BlockSpec(memory_space=pltpu.SMEM)
    vmem = pl.BlockSpec(memory_space=pltpu.VMEM)
    return pl.pallas_call(
        functools.partial(body, (ys, ks, rows, width, chunks)),
        out_shape=jax.ShapeDtypeStruct((rows, width), f32),
        in_specs=[anywhere, anywhere, scalars, vmem, scalars, scalars],
        out_specs=vmem,
        scratch_shapes=[
            pltpu.VMEM(blocks, f32),
            pltpu.VMEM(blocks, f32),
            pltpu.VMEM(peers, f32),
            pltpu.VMEM(peers, f32),
            pltpu.VMEM((ks, 2, width // LANES, LANES), f32),
            pltpu.VMEM((ks, chunks, 2, cols, LANES), f32),
            field, field, field, field, field,
            pltpu.VMEM((2, width // LANES, LANES), f32),
            pltpu.VMEM((2, SUB, LANES), f32),
            dma((ys, chunks, 2)),
            dma((ys, chunks, 2)),
            dma((ys, chunks, 2)),
            dma((ys - 1, chunks)),
            dma((ys - 1, chunks)),
            dma((ks - 1,)),
            dma((ks - 1,)),
            dma((ks - 1, chunks)),
            dma((ks - 1, chunks)),
            dma,
            dma,
        ],
        compiler_params=pltpu.CompilerParams(collective_id=0, has_side_effects=True),
    )(grad_part, illum_part, source_count, rate.reshape(1, -1), coef_table, coef_index)


def solution(mesh):
    placed = (
        P("shot", "depth", None),
        P("shot", "depth", None),
        P("shot"),
        P("shot"),
        P(),
        P("depth"),
    )
    return jax.shard_map(
        functools.partial(shards, mesh.shape["shot"] // 2, mesh.shape["depth"]),
        mesh=mesh, in_specs=placed, out_specs=P("depth", "shot"), check_vma=False,
    )
```

```python
import functools

import jax
import jax.numpy as jnp
from jax import lax
from jax.experimental import pallas as pl
from jax.experimental.pallas import tpu as pltpu
from jax.sharding import PartitionSpec as P

MESH = pl.DeviceIdType.MESH
LANES = 128
SUB = 8


def body(
    dims,
    grad, illum, weight, rate, table, index, out,
    own, part, sums, landed, early, late, inject, weigh, back, reach, held, states, theirs,
    own_sem, part_send, part_recv, sums_send, sums_recv,
    early_send, early_recv, late_send, late_recv, w_send, w_recv, word,
):
    ys, ks, rows, width, chunks = dims
    cw = width // chunks
    cols = cw // LANES
    tiles = rows // SUB
    me = lax.axis_index("shot")
    d = lax.axis_index("depth")
    y, c = me // 2, me % 2
    mate = y * 2 + 1 - c

    def peer(i):
        return lax.rem(d + i, ks)

    def other(i):
        return lax.rem(y + i, ys)

    def greet(semaphore):
        flip = d + 1 - 2 * lax.rem(d, 2)
        pl.semaphore_signal(semaphore, inc=1, device_id=(me, flip), device_id_type=MESH)
        for step in (2, -2):
            near = d + step

            @pl.when((near >= 0) & (near < ks))
            def _():
                pl.semaphore_signal(semaphore, inc=1, device_id=(me, near), device_id_type=MESH)

    def greeted(semaphore, more):
        inner = (d >= 2).astype(jnp.int32) + (d < ks - 2).astype(jnp.int32)
        pl.semaphore_wait(semaphore, inner + 1 + more)

    barrier = pltpu.get_barrier_semaphore()
    pl.semaphore_signal(barrier, inc=1, device_id=(mate, d), device_id_type=MESH)
    for i in range(1, ys):
        pl.semaphore_signal(barrier, inc=1, device_id=(other(i) * 2 + c, d), device_id_type=MESH)
    greet(barrier)

    def slab(src, target, core, ch):
        at = pl.multiple_of((target * 2 + core) * width + ch * cw, LANES)
        return src.at[0, :, pl.ds(at, cw)]

    order = [(i, ch) for i in [*range(1, ys), 0] for ch in range(chunks)]

    def own_copy(i, ch, a):
        return pltpu.make_async_copy(
            slab((grad, illum)[a], other(i), c, ch), own.at[i, ch, a], own_sem.at[i, ch, a]
        )

    def part_copy(i, ch, a):
        return pltpu.make_async_remote_copy(
            src_ref=slab((grad, illum)[a], other(i), 1 - c, ch),
            dst_ref=part.at[i, ch, a],
            send_sem=part_send.at[i, ch, a],
            recv_sem=part_recv.at[i, ch, a],
            device_id=(mate, d),
            device_id_type=MESH,
        )

    def sums_copy(i, ch):
        return pltpu.make_async_remote_copy(
            src_ref=sums.at[i - 1, ch],
            dst_ref=landed.at[i - 1, ch],
            send_sem=sums_send.at[i - 1, ch],
            recv_sem=sums_recv.at[i - 1, ch],
            device_id=(other(i) * 2 + c, d),
            device_id_type=MESH,
        )

    def early_copy(i):
        return pltpu.make_async_remote_copy(
            src_ref=early.at[0],
            dst_ref=early.at[ks - i],
            send_sem=early_send.at[i - 1],
            recv_sem=early_recv.at[ks - i - 1],
            device_id=(me, peer(i)),
            device_id_type=MESH,
        )

    def late_copy(i, ch):
        return pltpu.make_async_remote_copy(
            src_ref=late.at[0, ch],
            dst_ref=late.at[ks - i, ch],
            send_sem=late_send.at[i - 1, ch],
            recv_sem=late_recv.at[ks - i - 1, ch],
            device_id=(me, peer(i)),
            device_id_type=MESH,
        )

    w_copy = pltpu.make_async_remote_copy(
        src_ref=weight,
        dst_ref=theirs,
        send_sem=w_send,
        recv_sem=w_recv,
        device_id=(mate, d),
        device_id_type=MESH,
    )

    first_part, second_part = order[: (ys - 1) * chunks], order[(ys - 1) * chunks :]
    for i, ch in first_part:
        for a in range(2):
            own_copy(i, ch, a).start()

    greeted(barrier, ys)
    w_copy.start()
    for i, ch in first_part:
        for a in range(2):
            part_copy(i, ch, a).start()

    rounds = ks // 2 - 1
    greet(word.at[0])

    def pass_on(r):
        greeted(word.at[r], 0)
        if r + 1 < rounds:
            greet(word.at[r + 1])

    sub = lax.broadcasted_iota(jnp.int32, (SUB, LANES), 0)

    def prefix(v):
        for s in (1, 2, 4):
            v = v + jnp.where(sub >= s, pltpu.roll(v, s, 0), 0.0)
        return v

    def suffix(v):
        for s in (1, 2, 4):
            v = v + jnp.where(sub < SUB - s, pltpu.roll(v, SUB - s, 0), 0.0)
        return v

    def first(v):
        return jnp.broadcast_to(v[0:1], (SUB, LANES))

    def last(v):
        return jnp.broadcast_to(v[SUB - 1 : SUB], (SUB, LANES))

    entries = table.shape[1]

    def upright(row):
        n = row.shape[1]
        diagonal = lax.broadcasted_iota(jnp.int32, (n, n), 0) == lax.broadcasted_iota(
            jnp.int32, (n, n), 1
        )
        return jnp.sum(
            jnp.where(diagonal, jnp.broadcast_to(row, (n, n)), 0.0), axis=1, keepdims=True
        )

    level = lax.broadcasted_iota(jnp.int32, (entries, rows), 0)
    hit = jnp.broadcast_to(index[...], (entries, rows)) == level
    spread = jnp.broadcast_to(upright(table[...]), (entries, rows))
    picked = upright(jnp.sum(jnp.where(hit, spread, 0.0), axis=0, keepdims=True))

    coef, through, before = [], [], []
    total = jnp.zeros((SUB, LANES), jnp.float32)
    for t in range(tiles):
        v = jnp.broadcast_to(picked[t * SUB : (t + 1) * SUB], (SUB, LANES))
        run = prefix(v) + total
        coef.append(v)
        through.append(run)
        before.append(run - v)
        total = last(run)

    def terms():
        for j in range(width // LANES):
            at = pl.ds(j * LANES, LANES)
            ch, jj = j // cols, j % cols
            r = jnp.broadcast_to(rate[0:1, at], (SUB, LANES))
            tail = jnp.zeros((SUB, LANES), jnp.float32)
            for t in reversed(range(tiles)):
                zs = pl.ds(t * SUB, SUB)
                rest = 1.0 - jnp.exp(-(coef[t] * r))
                inject[zs, at] = rest * jnp.exp(through[t] * r)
                h = rest * jnp.exp(-((through[t] + before[t]) * r))
                weigh[zs, at] = h
                lift = jnp.exp(before[t] * r)
                back[zs, at] = lift
                run = suffix(h) + tail
                reach[zs, at] = lift * run
                tail = first(run)
            early[0, 0, pl.ds(j, 1), :] = jnp.exp(-(total * r))[0:1]
            early[0, 1, pl.ds(j, 1), :] = tail[0:1]

    def reduced(i, ch, a, zs, at):
        if a == 0:
            w, v = weight[...], theirs[...]
            return own[i, ch, 0, zs, at] * w + part[i, ch, 0, zs, at] * v
        return own[i, ch, 1, zs, at] + part[i, ch, 1, zs, at]

    def arrived(i, ch):
        for a in range(2):
            own_copy(i, ch, a).wait()
            part_copy(i, ch, a).wait_recv()

    w_copy.wait_recv()
    for n, (i, ch) in enumerate(first_part):
        arrived(i, ch)
        for j in range(cols):
            at = pl.ds(j * LANES, LANES)
            for t in range(tiles):
                zs = pl.ds(t * SUB, SUB)
                for a in range(2):
                    sums[i - 1, ch, a, zs, at] = reduced(i, ch, a, zs, at)
        sums_copy(i, ch).start()
        if n == 0:
            pass_on(0)

    for i, ch in second_part:
        for a in range(2):
            own_copy(i, ch, a).start()
            part_copy(i, ch, a).start()
    if rounds > 1:
        pass_on(1)
    terms()
    for r in range(2, rounds):
        pass_on(r)
    for i in range(1, ks):
        early_copy(i).start()

    for ch in range(chunks):
        arrived(0, ch)
        for i in range(1, ys):
            sums_copy(i, ch).wait_recv()
        for j in range(cols):
            at = pl.ds(j * LANES, LANES)
            full = pl.ds(ch * cw + j * LANES, LANES)
            carry = jnp.zeros((SUB, LANES), jnp.float32)
            parts = []
            for t in range(tiles):
                zs = pl.ds(t * SUB, SUB)
                num, den = reduced(0, ch, 0, zs, at), reduced(0, ch, 1, zs, at)
                for i in range(1, ys):
                    num = num + landed[i - 1, ch, 0, zs, at]
                    den = den + landed[i - 1, ch, 1, zs, at]
                run = prefix(inject[zs, full] * (num / den)) + carry
                parts.append(run)
                carry = last(run)
            row = pl.ds(ch * cols + j, 1)
            late[0, ch, 0, pl.ds(j, 1), :] = carry[0:1] * early[0, 0, row, :]
            tail = jnp.zeros((SUB, LANES), jnp.float32)
            for t in reversed(range(tiles)):
                zs = pl.ds(t * SUB, SUB)
                run = suffix(weigh[zs, full] * parts[t]) + tail
                held[zs, full] = run
                tail = first(run)
            late[0, ch, 1, pl.ds(j, 1), :] = tail[0:1]
        for i in range(1, ks):
            late_copy(i, ch).start()

    for i in range(1, ks):
        early_copy(i).wait_recv()

    for ch in range(chunks):
        for i in range(1, ks):
            late_copy(i, ch).wait_recv()
        rs = pl.ds(ch * cols, cols)
        state = jnp.zeros((cols, LANES), jnp.float32)
        mine = state
        ups = []
        for k in range(ks):
            slot = lax.rem(k - d + ks, ks)
            mine = jnp.where(k == d, state, mine)
            ups.append(late[slot, ch, 1] + early[slot, 1, rs] * state)
            if k < ks - 1:
                state = late[slot, ch, 0] + early[slot, 0, rs] * state
        up = jnp.zeros((cols, LANES), jnp.float32)
        for k in reversed(range(1, ks)):
            slot = lax.rem(k - d + ks, ks)
            up = jnp.where(k > d, ups[k] + early[slot, 0, rs] * up, up)
        states[0, rs] = mine
        states[1, rs] = up * early[0, 0, rs]
        for j in range(cols):
            row = pl.ds(ch * cols + j, 1)
            full = pl.ds(ch * cw + j * LANES, LANES)
            e = jnp.broadcast_to(states[0, row, :], (SUB, LANES))
            b = jnp.broadcast_to(states[1, row, :], (SUB, LANES))
            for t in range(tiles):
                zs = pl.ds(t * SUB, SUB)
                out[zs, full] = back[zs, full] * (held[zs, full] + b) + reach[zs, full] * e

    w_copy.wait_send()
    for i, ch in order:
        for a in range(2):
            part_copy(i, ch, a).wait_send()
        if i:
            sums_copy(i, ch).wait_send()
    for i in range(1, ks):
        early_copy(i).wait_send()
        for ch in range(chunks):
            late_copy(i, ch).wait_send()


def shards(ys, ks, grad_part, illum_part, source_count, rate, coef_table, coef_index):
    _, rows, lateral = grad_part.shape
    width = lateral // (2 * ys)
    chunks = min(2, width // LANES)
    cw = width // chunks
    cols = cw // LANES
    f32 = jnp.float32
    dma = pltpu.SemaphoreType.DMA
    blocks = (ys, chunks, 2, rows, cw)
    peers = (ys - 1, chunks, 2, rows, cw)
    field = pltpu.VMEM((rows, width), f32)
    anywhere = pl.BlockSpec(memory_space=pl.ANY)
    vmem = pl.BlockSpec(memory_space=pltpu.VMEM)
    return pl.pallas_call(
        functools.partial(body, (ys, ks, rows, width, chunks)),
        out_shape=jax.ShapeDtypeStruct((rows, width), f32),
        in_specs=[anywhere, anywhere, vmem, vmem, vmem, vmem],
        out_specs=vmem,
        scratch_shapes=[
            pltpu.VMEM(blocks, f32),
            pltpu.VMEM(blocks, f32),
            pltpu.VMEM(peers, f32),
            pltpu.VMEM(peers, f32),
            pltpu.VMEM((ks, 2, width // LANES, LANES), f32),
            pltpu.VMEM((ks, chunks, 2, cols, LANES), f32),
            field, field, field, field, field,
            pltpu.VMEM((2, width // LANES, LANES), f32),
            pltpu.VMEM((SUB, LANES), f32),
            dma((ys, chunks, 2)),
            dma((ys, chunks, 2)),
            dma((ys, chunks, 2)),
            dma((ys - 1, chunks)),
            dma((ys - 1, chunks)),
            dma((ks - 1,)),
            dma((ks - 1,)),
            dma((ks - 1, chunks)),
            dma((ks - 1, chunks)),
            dma,
            dma,
            pltpu.SemaphoreType.REGULAR((ks // 2 - 1,)),
        ],
        compiler_params=pltpu.CompilerParams(collective_id=0, has_side_effects=True, vmem_limit_bytes=53 * 2**20),
    )(
        grad_part,
        illum_part,
        jnp.broadcast_to(1.0 / source_count.astype(f32)[:, None], (SUB, LANES)),
        rate.reshape(1, -1),
        coef_table.reshape(1, -1),
        coef_index.reshape(1, -1),
    )


def solution(mesh):
    placed = (
        P("shot", "depth", None),
        P("shot", "depth", None),
        P("shot"),
        P("shot"),
        P(),
        P("depth"),
    )
    return jax.shard_map(
        functools.partial(shards, mesh.shape["shot"] // 2, mesh.shape["depth"]),
        mesh=mesh, in_specs=placed, out_specs=P("depth", "shot"), check_vma=False,
    )
```

```python
import functools

import jax
import jax.numpy as jnp
from jax import lax
from jax.experimental import pallas as pl
from jax.experimental.pallas import tpu as pltpu
from jax.sharding import PartitionSpec as P

MESH = pl.DeviceIdType.MESH
LANES = 128
SUB = 8


def body(
    dims,
    grad, illum, weight, rate, table, index, out,
    own, part, sums, landed, early, late, inject, weigh, back, reach, held, states, theirs,
    own_sem, part_send, part_recv, sums_send, sums_recv,
    early_send, early_recv, late_send, late_recv, w_send, w_recv, word,
):
    ys, ks, rows, width, counts = dims
    chunks = len(counts)
    starts = [sum(counts[:ch]) for ch in range(chunks)]
    tiles = rows // SUB
    me = lax.axis_index("shot")
    d = lax.axis_index("depth")
    y, c = me // 2, me % 2
    mate = y * 2 + 1 - c

    def peer(i):
        return lax.rem(d + i, ks)

    def other(i):
        return lax.rem(y + i, ys)

    def greet(semaphore):
        flip = d + 1 - 2 * lax.rem(d, 2)
        pl.semaphore_signal(semaphore, inc=1, device_id=(me, flip), device_id_type=MESH)
        for step in (2, -2):
            near = d + step

            @pl.when((near >= 0) & (near < ks))
            def _():
                pl.semaphore_signal(semaphore, inc=1, device_id=(me, near), device_id_type=MESH)

    def greeted(semaphore, more):
        inner = (d >= 2).astype(jnp.int32) + (d < ks - 2).astype(jnp.int32)
        pl.semaphore_wait(semaphore, inner + 1 + more)

    barrier = pltpu.get_barrier_semaphore()
    pl.semaphore_signal(barrier, inc=1, device_id=(mate, d), device_id_type=MESH)
    for i in range(1, ys):
        pl.semaphore_signal(barrier, inc=1, device_id=(other(i) * 2 + c, d), device_id_type=MESH)
    greet(barrier)

    def slab(src, target, core, ch):
        at = pl.multiple_of((target * 2 + core) * width + starts[ch] * LANES, LANES)
        return src.at[0, :, pl.ds(at, counts[ch] * LANES)]

    def span(ch):
        return pl.ds(0, counts[ch] * LANES)

    order = [(i, ch) for i in [*range(1, ys), 0] for ch in range(chunks)]

    def own_copy(i, ch, a):
        return pltpu.make_async_copy(
            slab((grad, illum)[a], other(i), c, ch), own.at[i, ch, a, :, span(ch)], own_sem.at[i, ch, a]
        )

    def part_copy(i, ch, a):
        return pltpu.make_async_remote_copy(
            src_ref=slab((grad, illum)[a], other(i), 1 - c, ch),
            dst_ref=part.at[i, ch, a, :, span(ch)],
            send_sem=part_send.at[i, ch, a],
            recv_sem=part_recv.at[i, ch, a],
            device_id=(mate, d),
            device_id_type=MESH,
        )

    def sums_copy(i, ch):
        return pltpu.make_async_remote_copy(
            src_ref=sums.at[i - 1, ch, :, :, span(ch)],
            dst_ref=landed.at[i - 1, ch, :, :, span(ch)],
            send_sem=sums_send.at[i - 1, ch],
            recv_sem=sums_recv.at[i - 1, ch],
            device_id=(other(i) * 2 + c, d),
            device_id_type=MESH,
        )

    def early_copy(i):
        return pltpu.make_async_remote_copy(
            src_ref=early.at[0],
            dst_ref=early.at[ks - i],
            send_sem=early_send.at[i - 1],
            recv_sem=early_recv.at[ks - i - 1],
            device_id=(me, peer(i)),
            device_id_type=MESH,
        )

    def late_copy(i, ch):
        return pltpu.make_async_remote_copy(
            src_ref=late.at[0, ch],
            dst_ref=late.at[ks - i, ch],
            send_sem=late_send.at[i - 1, ch],
            recv_sem=late_recv.at[ks - i - 1, ch],
            device_id=(me, peer(i)),
            device_id_type=MESH,
        )

    w_copy = pltpu.make_async_remote_copy(
        src_ref=weight,
        dst_ref=theirs,
        send_sem=w_send,
        recv_sem=w_recv,
        device_id=(mate, d),
        device_id_type=MESH,
    )

    first_part, second_part = order[: (ys - 1) * chunks], order[(ys - 1) * chunks :]
    for i, ch in first_part:
        for a in range(2):
            own_copy(i, ch, a).start()

    greeted(barrier, ys)
    w_copy.start()
    for i, ch in first_part:
        for a in range(2):
            part_copy(i, ch, a).start()

    rounds = ks // 2 - 1
    greet(word.at[0])

    def pass_on(r):
        greeted(word.at[r], 0)
        if r + 1 < rounds:
            greet(word.at[r + 1])

    sub = lax.broadcasted_iota(jnp.int32, (SUB, LANES), 0)

    def prefix(v):
        for s in (1, 2, 4):
            v = v + jnp.where(sub >= s, pltpu.roll(v, s, 0), 0.0)
        return v

    def suffix(v):
        for s in (1, 2, 4):
            v = v + jnp.where(sub < SUB - s, pltpu.roll(v, SUB - s, 0), 0.0)
        return v

    def first(v):
        return jnp.broadcast_to(v[0:1], (SUB, LANES))

    def last(v):
        return jnp.broadcast_to(v[SUB - 1 : SUB], (SUB, LANES))

    entries = table.shape[1]

    def upright(row):
        n = row.shape[1]
        diagonal = lax.broadcasted_iota(jnp.int32, (n, n), 0) == lax.broadcasted_iota(
            jnp.int32, (n, n), 1
        )
        return jnp.sum(
            jnp.where(diagonal, jnp.broadcast_to(row, (n, n)), 0.0), axis=1, keepdims=True
        )

    level = lax.broadcasted_iota(jnp.int32, (entries, rows), 0)
    hit = jnp.broadcast_to(index[...], (entries, rows)) == level
    spread = jnp.broadcast_to(upright(table[...]), (entries, rows))
    picked = upright(jnp.sum(jnp.where(hit, spread, 0.0), axis=0, keepdims=True))

    coef, through, before = [], [], []
    total = jnp.zeros((SUB, LANES), jnp.float32)
    for t in range(tiles):
        v = jnp.broadcast_to(picked[t * SUB : (t + 1) * SUB], (SUB, LANES))
        run = prefix(v) + total
        coef.append(v)
        through.append(run)
        before.append(run - v)
        total = last(run)

    def terms():
        for j in range(width // LANES):
            at = pl.ds(j * LANES, LANES)
            r = jnp.broadcast_to(rate[0:1, at], (SUB, LANES))
            tail = jnp.zeros((SUB, LANES), jnp.float32)
            for t in reversed(range(tiles)):
                zs = pl.ds(t * SUB, SUB)
                rest = 1.0 - jnp.exp(-(coef[t] * r))
                inject[zs, at] = rest * jnp.exp(through[t] * r)
                h = rest * jnp.exp(-((through[t] + before[t]) * r))
                weigh[zs, at] = h
                lift = jnp.exp(before[t] * r)
                back[zs, at] = lift
                run = suffix(h) + tail
                reach[zs, at] = lift * run
                tail = first(run)
            early[0, 0, pl.ds(j, 1), :] = jnp.exp(-(total * r))[0:1]
            early[0, 1, pl.ds(j, 1), :] = tail[0:1]

    def reduced(i, ch, a, zs, at):
        if a == 0:
            w, v = weight[...], theirs[...]
            return own[i, ch, 0, zs, at] * w + part[i, ch, 0, zs, at] * v
        return own[i, ch, 1, zs, at] + part[i, ch, 1, zs, at]

    def arrived(i, ch):
        for a in range(2):
            own_copy(i, ch, a).wait()
            part_copy(i, ch, a).wait_recv()

    w_copy.wait_recv()
    for n, (i, ch) in enumerate(first_part):
        arrived(i, ch)
        for j in range(counts[ch]):
            at = pl.ds(j * LANES, LANES)
            for t in range(tiles):
                zs = pl.ds(t * SUB, SUB)
                for a in range(2):
                    sums[i - 1, ch, a, zs, at] = reduced(i, ch, a, zs, at)
        sums_copy(i, ch).start()
        if n == 0:
            pass_on(0)

    for i, ch in second_part:
        for a in range(2):
            own_copy(i, ch, a).start()
            part_copy(i, ch, a).start()
    if rounds > 1:
        pass_on(1)
    terms()
    for r in range(2, rounds):
        pass_on(r)
    for i in range(1, ks):
        early_copy(i).start()

    for ch in range(chunks):
        arrived(0, ch)
        for i in range(1, ys):
            sums_copy(i, ch).wait_recv()
        for j in range(counts[ch]):
            at = pl.ds(j * LANES, LANES)
            full = pl.ds((starts[ch] + j) * LANES, LANES)
            carry = jnp.zeros((SUB, LANES), jnp.float32)
            parts = []
            for t in range(tiles):
                zs = pl.ds(t * SUB, SUB)
                num, den = reduced(0, ch, 0, zs, at), reduced(0, ch, 1, zs, at)
                for i in range(1, ys):
                    num = num + landed[i - 1, ch, 0, zs, at]
                    den = den + landed[i - 1, ch, 1, zs, at]
                run = prefix(inject[zs, full] * (num / den)) + carry
                parts.append(run)
                carry = last(run)
            row = pl.ds(starts[ch] + j, 1)
            late[0, ch, 0, pl.ds(j, 1), :] = carry[0:1] * early[0, 0, row, :]
            tail = jnp.zeros((SUB, LANES), jnp.float32)
            for t in reversed(range(tiles)):
                zs = pl.ds(t * SUB, SUB)
                run = suffix(weigh[zs, full] * parts[t]) + tail
                held[zs, full] = run
                tail = first(run)
            late[0, ch, 1, pl.ds(j, 1), :] = tail[0:1]
        for i in range(1, ks):
            late_copy(i, ch).start()

    for i in range(1, ks):
        early_copy(i).wait_recv()

    for ch in range(chunks):
        for i in range(1, ks):
            late_copy(i, ch).wait_recv()
        cols = counts[ch]
        rs = pl.ds(starts[ch], cols)
        state = jnp.zeros((cols, LANES), jnp.float32)
        mine = state
        ups = []
        for k in range(ks):
            slot = lax.rem(k - d + ks, ks)
            mine = jnp.where(k == d, state, mine)
            ups.append(late[slot, ch, 1, :cols] + early[slot, 1, rs] * state)
            if k < ks - 1:
                state = late[slot, ch, 0, :cols] + early[slot, 0, rs] * state
        up = jnp.zeros((cols, LANES), jnp.float32)
        for k in reversed(range(1, ks)):
            slot = lax.rem(k - d + ks, ks)
            up = jnp.where(k > d, ups[k] + early[slot, 0, rs] * up, up)
        states[0, rs] = mine
        states[1, rs] = up * early[0, 0, rs]
        for j in range(counts[ch]):
            row = pl.ds(starts[ch] + j, 1)
            full = pl.ds((starts[ch] + j) * LANES, LANES)
            e = jnp.broadcast_to(states[0, row, :], (SUB, LANES))
            b = jnp.broadcast_to(states[1, row, :], (SUB, LANES))
            for t in range(tiles):
                zs = pl.ds(t * SUB, SUB)
                out[zs, full] = back[zs, full] * (held[zs, full] + b) + reach[zs, full] * e

    w_copy.wait_send()
    for i, ch in order:
        for a in range(2):
            part_copy(i, ch, a).wait_send()
        if i:
            sums_copy(i, ch).wait_send()
    for i in range(1, ks):
        early_copy(i).wait_send()
        for ch in range(chunks):
            late_copy(i, ch).wait_send()


def shards(ys, ks, grad_part, illum_part, source_count, rate, coef_table, coef_index):
    _, rows, lateral = grad_part.shape
    width = lateral // (2 * ys)
    blocks_across = width // LANES
    lead = max(1, blocks_across // 8)
    half = blocks_across // 2
    counts = (lead, half, blocks_across - lead - half)
    chunks, cols = len(counts), half
    cw = cols * LANES
    f32 = jnp.float32
    dma = pltpu.SemaphoreType.DMA
    blocks = (ys, chunks, 2, rows, cw)
    peers = (ys - 1, chunks, 2, rows, cw)
    field = pltpu.VMEM((rows, width), f32)
    anywhere = pl.BlockSpec(memory_space=pl.ANY)
    vmem = pl.BlockSpec(memory_space=pltpu.VMEM)
    return pl.pallas_call(
        functools.partial(body, (ys, ks, rows, width, counts)),
        out_shape=jax.ShapeDtypeStruct((rows, width), f32),
        in_specs=[anywhere, anywhere, vmem, vmem, vmem, vmem],
        out_specs=vmem,
        scratch_shapes=[
            pltpu.VMEM(blocks, f32),
            pltpu.VMEM(blocks, f32),
            pltpu.VMEM(peers, f32),
            pltpu.VMEM(peers, f32),
            pltpu.VMEM((ks, 2, width // LANES, LANES), f32),
            pltpu.VMEM((ks, chunks, 2, cols, LANES), f32),
            field, field, field, field, field,
            pltpu.VMEM((2, width // LANES, LANES), f32),
            pltpu.VMEM((SUB, LANES), f32),
            dma((ys, chunks, 2)),
            dma((ys, chunks, 2)),
            dma((ys, chunks, 2)),
            dma((ys - 1, chunks)),
            dma((ys - 1, chunks)),
            dma((ks - 1,)),
            dma((ks - 1,)),
            dma((ks - 1, chunks)),
            dma((ks - 1, chunks)),
            dma,
            dma,
            pltpu.SemaphoreType.REGULAR((ks // 2 - 1,)),
        ],
        compiler_params=pltpu.CompilerParams(collective_id=0, has_side_effects=True, vmem_limit_bytes=53 * 2**20),
    )(
        grad_part,
        illum_part,
        jnp.broadcast_to(1.0 / source_count.astype(f32)[:, None], (SUB, LANES)),
        rate.reshape(1, -1),
        coef_table.reshape(1, -1),
        coef_index.reshape(1, -1),
    )


def solution(mesh):
    placed = (
        P("shot", "depth", None),
        P("shot", "depth", None),
        P("shot"),
        P("shot"),
        P(),
        P("depth"),
    )
    return jax.shard_map(
        functools.partial(shards, mesh.shape["shot"] // 2, mesh.shape["depth"]),
        mesh=mesh, in_specs=placed, out_specs=P("depth", "shot"), check_vma=False,
    )
```
